32 devices in a mesh: sweep: 16 (over z, y, x), cols: 2 (over core).
Axes of the slice: x: 2, y: 2, z: 4, core: 2. Of those that a mesh axis runs over, the one named last changes fastest.
Arguments:
- rhs: bfloat16 [4, 16, 256, 1024], P(None, 'sweep', None, 'cols'), may hold values from -6 to 6
- blocks: bfloat16 [3, 16, 6, 256, 256], P(None, 'sweep', None, 'cols'), may hold values from -0.1875 to 0.1875
- diag_inv: bfloat16 [4, 16, 256, 256], P(None, 'sweep', 'cols'), as said below
- neighbours: int32 [3, 16, 6], P(None, 'sweep'), may hold values from -1 to 47, as said below
Outputs:
- samples: bfloat16 [4, 16, 256, 1024], P(None, 'sweep', None, 'cols')
The draws below stay inside these ranges and needn't reach their ends.
Inputs may be any that keep to these rules, and one draw needn't show every extreme that they name: neighbours[b, p, k] belongs to block row (b + 1, p): -1 marks an unused slot; a used slot names block row b * 16 + p - o for some o with 0 <= o <= min(5, p), and the used slots of one block row name distinct rows. The last owner's block rows use all 6 slots. `diag_inv`: every block is lower triangular with a positive diagonal.
All inputs are finite; a program needn't handle non-finite values.
Results may differ from the reference program's by a relative error of at most 0.0095.
Values may be sent and summed in bfloat16 or wider, within the bound.
A program may use at most 64 MiB of HBM per device.

```python
import math
import jax
import jax.numpy as jnp
from jax import lax

BS = 256
LEVELS = 4
KMAX = 6
REACH = 5
OWNERS = 16
NCOL = 1024


def draw_neighbours(key, part):
    key_perm, key_cap, key_count = jax.random.split(jax.random.fold_in(key, 11), 3)
    total_rows = (LEVELS - 1) * OWNERS
    row_keys = jax.random.split(key_perm, total_rows)
    perms = jax.vmap(lambda row_key: jax.random.permutation(row_key, REACH + 1))(row_keys)
    perms = perms[:, :KMAX].reshape(LEVELS - 1, OWNERS, KMAX).astype(jnp.int32)
    caps = jax.random.randint(key_cap, (OWNERS,), 1, KMAX + 1)
    counts = jax.random.randint(key_count, (LEVELS - 1, OWNERS), 1, caps[None, :] + 1)
    owner = jnp.arange(OWNERS, dtype=jnp.int32)[None, :]
    counts = jnp.where(owner == OWNERS - 1, KMAX, counts)
    slot = jnp.arange(KMAX, dtype=jnp.int32)[None, None, :]
    level = jnp.arange(LEVELS - 1, dtype=jnp.int32)[:, None, None]
    used = (slot < counts[:, :, None]) & (perms <= owner[:, :, None])
    return jnp.where(used, level * OWNERS + owner[:, :, None] - perms, -1).astype(jnp.int32)


def draw_diag_inv(key, part):
    key_off, key_diag = jax.random.split(jax.random.fold_in(key, 23))
    shape = (LEVELS, OWNERS, BS, BS)
    offdiag = jax.random.normal(key_off, shape, jnp.float32) / math.sqrt(BS)
    diagonal = jnp.exp(jax.random.uniform(key_diag, (LEVELS, OWNERS, BS), jnp.float32, math.log(0.5), math.log(2.0)))
    rows = jnp.arange(BS)[:, None]
    cols = jnp.arange(BS)[None, :]
    lower = jnp.where(rows > cols, offdiag, 0.0)
    eye = (rows == cols).astype(jnp.float32)
    return (lower + diagonal[..., None] * eye).astype(jnp.bfloat16)


def steps_of(key, shape, shards, smallest, largest):
    loudness, own = 1.0, jax.random.fold_in(key, 6)
    for dim, blocks in shards:
        heights = jnp.exp(jax.random.uniform(jax.random.fold_in(own, dim), (blocks,), jnp.float32, smallest / len(shards), largest / len(shards)))
        loudness = loudness * jnp.repeat(heights, shape[dim] // blocks).reshape([-1 if axis == dim else 1 for axis in range(len(shape))])
    return loudness


def gaussian(key, dims, scale, reach, cuts=(), kind=jnp.bfloat16):
    loudness = steps_of(key, dims, cuts, -0.22, 0.18) if cuts else 1.0
    result = jax.random.normal(key, dims, jnp.float32) * scale * loudness
    return jnp.minimum(jnp.maximum(result, -reach), reach).astype(kind)


def setup_inputs(seed: int = 0) -> dict:
    keys = jax.random.split(jax.random.key(seed), 5)
    return {
        "rhs": gaussian(keys[0], (LEVELS, OWNERS, BS, NCOL), 1.0, 6.0, ((1, 16), (3, 2))),
        "blocks": gaussian(keys[1], (LEVELS - 1, OWNERS, KMAX, BS, BS), (4 * BS) ** -0.5, 0.1875, ((1, 16), (3, 2))),
        "diag_inv": draw_diag_inv(jax.random.fold_in(keys[4], 71), 0),
        "neighbours": draw_neighbours(jax.random.fold_in(keys[4], 71), 0),
    }


def reference(rhs, blocks, diag_inv, neighbours):
    owners = rhs.shape[1]
    solved = [jnp.einsum('pab,pbc->pac', diag_inv[0].astype(jnp.float32), rhs[0].astype(jnp.float32)).astype(jnp.bfloat16)]
    for level in range(1, LEVELS):
        row_ids = neighbours[level - 1]
        valid = (row_ids >= 0).astype(jnp.float32)
        local = jnp.clip(row_ids - (level - 1) * owners, 0, owners - 1).astype(jnp.int32)
        sums = jnp.zeros(rhs.shape[1:], jnp.float32)
        for slot in range(KMAX):
            picked = solved[level - 1][local[:, slot]].astype(jnp.float32) * valid[:, slot][:, None, None]
            sums = sums + jnp.einsum('pab,pbc->pac', blocks[level - 1, :, slot].astype(jnp.float32), picked)
        residue = (rhs[level].astype(jnp.float32) - sums).astype(jnp.bfloat16)
        solved.append(jnp.einsum('pab,pbc->pac', diag_inv[level].astype(jnp.float32), residue.astype(jnp.float32)).astype(jnp.bfloat16))
    top = LEVELS - 1
    samples = [None] * LEVELS
    samples[top] = jnp.einsum('pba,pbc->pac', diag_inv[top].astype(jnp.float32), solved[top].astype(jnp.float32)).astype(jnp.bfloat16)
    for level in range(LEVELS - 2, -1, -1):
        row_ids = neighbours[level]
        valid = (row_ids >= 0).astype(jnp.float32)
        local = jnp.clip(row_ids - level * owners, 0, owners - 1).astype(jnp.int32)
        upper = samples[level + 1].astype(jnp.float32)
        back_terms = jnp.zeros(rhs.shape[1:], jnp.float32)
        for slot in range(KMAX):
            term = jnp.einsum('pba,pbc->pac', blocks[level, :, slot].astype(jnp.float32), upper) * valid[:, slot][:, None, None]
            term = lax.optimization_barrier(term.astype(jnp.bfloat16)).astype(jnp.float32)
            back_terms = back_terms.at[local[:, slot]].add(term)
        adjusted = (solved[level].astype(jnp.float32) - back_terms).astype(jnp.bfloat16)
        samples[level] = jnp.einsum('pba,pbc->pac', diag_inv[level].astype(jnp.float32), adjusted.astype(jnp.float32)).astype(jnp.bfloat16)
    return jnp.stack(samples)
```

```python
import functools

import jax
import jax.numpy as jnp
from jax import lax
from jax.experimental import pallas as pl
from jax.experimental.pallas import tpu as pltpu
from jax.sharding import PartitionSpec as P

REACH = 5
GROUP = 4
F32 = jnp.float32
BF16 = jnp.bfloat16


def mm(a, b):
    return jnp.dot(a, b, preferred_element_type=F32)


def kernel(
    owners, ncores, nbr, rhs, blocks, diag, out,
    fac, win, rloc, solved_t, samp_t, near, far, stage, ostage,
    s_own, r_own, s_dg, r_dg, s_core, r_core, s_rhs, r_rhs, s_loc,
    s_x, r_x, s_b, r_b, s_o, r_o,
):
    levels = rhs.shape[0]
    rows = diag.shape[2]
    width = rhs.shape[3] // GROUP
    planes = owners // GROUP
    me = lax.axis_index("sweep")
    c = lax.axis_index("cols")
    k = me // GROUP
    i = me % GROUP
    px = i + 1 - 2 * (i % 2)
    py = (i + 2) % GROUP
    dg = GROUP - 1 - i
    base = k * GROUP
    peers = (px, py, dg)

    def at(owner, core):
        return (owner, core)

    def remote(src, dst, ssem, rsem, dev):
        return pltpu.make_async_remote_copy(
            src_ref=src, dst_ref=dst, send_sem=ssem, recv_sem=rsem,
            device_id=dev, device_id_type=pl.DeviceIdType.MESH,
        )

    win[:, 0:REACH] = jnp.zeros((levels - 1, REACH) + win.shape[2:], BF16)
    near[...] = jnp.zeros_like(near)
    far[...] = jnp.zeros_like(far)

    barrier = pltpu.get_barrier_semaphore()

    def greet(owner, core):
        pl.semaphore_signal(
            barrier, inc=1, device_id=at(owner, core), device_id_type=pl.DeviceIdType.MESH
        )

    for q in peers:
        greet(base + q, c)
    for r in range(1, ncores):
        greet(me, (c + r) % ncores)
    count = 3 + ncores - 1
    for d in (1, 2):
        @pl.when(k >= d)
        def _():
            greet(me - d * GROUP, c)

        @pl.when(k + d < planes)
        def _():
            greet(me + d * GROUP, c)

        count = count + jnp.where(k >= d, 1, 0) + jnp.where(k + d < planes, 1, 0)

    mine = pl.ds(pl.multiple_of(c * rows, rows), rows)
    for t in range(levels):
        fac[t, i, REACH + 1, mine, :] = diag[t, 0]
    for l in range(levels - 1):
        for o in range(REACH + 1):
            slot, hit = jnp.int32(0), jnp.int32(0)
            for s in range(blocks.shape[2]):
                got = nbr[l, s]
                same = (got == l * owners + me - o) & (got >= 0)
                slot = jnp.where(same, s, slot)
                hit = jnp.where(same, 1, hit)
            block = blocks[l, 0, slot].astype(F32) * hit.astype(F32)
            fac[l + 1, i, o, mine, :] = block.astype(BF16)

    pl.semaphore_wait(barrier, count)

    half = rows // 2

    def shard(t, owner):
        first = REACH + 1 if t == 0 else 0
        return fac.at[t, owner, pl.ds(first, REACH + 2 - first), mine, :]

    def shard_half(t, owner, h):
        first = REACH + 1 if t == 0 else 0
        part = pl.ds(pl.multiple_of(c * rows + h * half, half), half)
        return fac.at[t, owner, pl.ds(first, REACH + 2 - first), part, :]

    def own_copy(t, n):
        ref = shard(t, i)
        return remote(ref, ref, s_own.at[t, n], r_own.at[t, n], at(base + peers[n], c))

    def diag_copy(t, n):
        ref = shard_half(t, peers[n], n)
        return remote(ref, ref, s_dg.at[t, n], r_dg.at[t, n], at(base + peers[1 - n], c))

    def core_copy(t, source, r):
        ref = shard(t, ((i,) + peers)[source])
        return remote(
            ref, ref, s_core.at[t, source, r - 1], r_core.at[t, source, r - 1],
            at(me, (c + r) % ncores),
        )

    def rhs_copy(t, n):
        q = peers[n]
        cols = pl.ds(pl.multiple_of(q * width, width), width)
        return remote(
            rhs.at[t, 0, :, cols], rloc.at[t, i], s_rhs.at[t, n], r_rhs.at[t, n], at(base + q, c)
        )

    def rhs_local(t):
        cols = pl.ds(pl.multiple_of(i * width, width), width)
        return pltpu.make_async_copy(rhs.at[t, 0, :, cols], rloc.at[t, i], s_loc.at[t])

    cores = range(1, ncores)

    def start(t):
        for n in range(3):
            rhs_copy(t, n).start()
        rhs_local(t).start()
        for n in range(2):
            own_copy(t, n).start()
        for r in cores:
            core_copy(t, 0, r).start()

    def forward(t):
        for n in range(2):
            own_copy(t, n).wait_recv()
            diag_copy(t, n).start()
            for r in cores:
                core_copy(t, 1 + n, r).start()

    def finish_diag(t):
        for n in range(2):
            diag_copy(t, n).wait_recv()
        for r in cores:
            core_copy(t, 3, r).start()

    def arrived(t):
        for n in range(3):
            rhs_copy(t, n).wait_recv()
        rhs_local(t).wait()
        for source in range(4):
            for r in cores:
                core_copy(t, source, r).wait_recv()

    def sent(t):
        for n in range(3):
            rhs_copy(t, n).wait_send()
        for n in range(2):
            own_copy(t, n).wait_send()
            diag_copy(t, n).wait_send()
        for source in range(4):
            for r in cores:
                core_copy(t, source, r).wait_send()

    def solved_copy(l, n):
        j = GROUP - 1 if n == GROUP else n
        step, spot = (2, 0) if n == GROUP else (1, 1 + n)
        return remote(
            win.at[l, REACH + j], win.at[l, spot], s_x.at[l, n], r_x.at[l, n],
            at(me + step * GROUP, c),
        )

    def solve(l):
        for j in reversed(range(GROUP)):
            res = rloc[l, j]
            if l > 0:
                acc = mm(fac[l, j, 0], win[l - 1, REACH + j])
                for o in range(1, REACH + 1):
                    acc = acc + mm(fac[l, j, o], win[l - 1, REACH + j - o])
                res = (res.astype(F32) - acc).astype(BF16)
            y = mm(fac[l, j, REACH + 1], res)
            if l < levels - 1:
                win[l, REACH + j] = y.astype(BF16)

                @pl.when(k + 1 < planes)
                def _():
                    solved_copy(l, j).start()

                if j == GROUP - 1:
                    @pl.when(k + 2 < planes)
                    def _():
                        solved_copy(l, GROUP).start()

            solved_t[l, j] = y.T.astype(BF16)

    def solved_recv(l):
        @pl.when(k >= 1)
        def _():
            for n in range(GROUP):
                solved_copy(l, n).wait_recv()

        @pl.when(k >= 2)
        def _():
            solved_copy(l, GROUP).wait_recv()

    start(0)
    start(1)
    forward(0)
    if levels > 2:
        start(2)
    finish_diag(0)
    for l in range(levels):
        if l + 1 < levels:
            forward(l + 1)
        if l + 3 < levels:
            start(l + 3)
        arrived(l)
        if l > 0:
            solved_recv(l - 1)
        solve(l)
        if l + 1 < levels:
            finish_diag(l + 1)

    def term_copy(l, n):
        step, dst = (2, far.at[l]) if n == 0 else (1, near.at[l, n - 1])
        return remote(
            stage.at[l, n], dst, s_b.at[l, n], r_b.at[l, n], at(me - step * GROUP, c)
        )

    def out_copy(l, n):
        q = peers[n]
        cols = pl.ds(pl.multiple_of(i * width, width), width)
        return remote(
            ostage.at[l, q], out.at[l, 0, :, cols], s_o.at[l, n], r_o.at[l, n], at(base + q, c)
        )

    def out_local(l):
        cols = pl.ds(pl.multiple_of(i * width, width), width)
        return pltpu.make_async_copy(ostage.at[l, i], out.at[l, 0, :, cols], s_o.at[l, 3])

    def finish_level(l, adjusted):
        for j in range(GROUP):
            samp_t[l, j] = mm(adjusted[j], fac[l, j, REACH + 1]).astype(BF16)

    def emit(l):
        for j in range(GROUP):
            ostage[l, j] = samp_t[l, j].astype(F32).T.astype(BF16)
        for n in range(3):
            out_copy(l, n).start()
        out_local(l).start()

    def terms(l, w):
        total = None
        for j in range(max(0, w - REACH), min(GROUP - 1, w) + 1):
            term = mm(samp_t[l + 1, j], fac[l + 1, j, REACH + j - w])
            total = term if total is None else total + term
        return total

    top = levels - 1
    finish_level(top, [solved_t[top, j] for j in range(GROUP)])
    for l in range(levels - 2, -1, -1):
        for w in range(REACH):
            stage[l, w] = terms(l, w).astype(BF16)
            step = 2 if w == 0 else 1

            @pl.when(k >= step)
            def _():
                term_copy(l, w).start()

        emit(l + 1)
        back = [terms(l, REACH + j) for j in range(GROUP)]

        @pl.when(k + 1 < planes)
        def _():
            for n in range(1, REACH):
                term_copy(l, n).wait_recv()

        @pl.when(k + 2 < planes)
        def _():
            term_copy(l, 0).wait_recv()

        adjusted = []
        for j in range(GROUP):
            total = back[j] + near[l, j].astype(F32)
            if j == GROUP - 1:
                total = total + far[l].astype(F32)
            adjusted.append((solved_t[l, j].astype(F32) - total).astype(BF16))
        finish_level(l, adjusted)
    emit(0)

    for t in range(levels):
        sent(t)
    for l in range(levels - 1):
        @pl.when(k + 1 < planes)
        def _():
            for n in range(GROUP):
                solved_copy(l, n).wait_send()

        @pl.when(k + 2 < planes)
        def _():
            solved_copy(l, GROUP).wait_send()

        @pl.when(k >= 1)
        def _():
            for n in range(1, REACH):
                term_copy(l, n).wait_send()

        @pl.when(k >= 2)
        def _():
            term_copy(l, 0).wait_send()

    for l in range(levels):
        for n in range(3):
            out_copy(l, n).wait()
        out_local(l).wait()


def on_device(rhs, blocks, diag_inv, neighbours):
    owners = lax.axis_size("sweep")
    ncores = lax.axis_size("cols")
    levels, _, bs, cols = rhs.shape
    width = cols // GROUP
    dma = pltpu.SemaphoreType.DMA
    vmem = pl.BlockSpec(memory_space=pltpu.VMEM)
    return pl.pallas_call(
        functools.partial(kernel, owners, ncores),
        out_shape=jax.ShapeDtypeStruct(rhs.shape, rhs.dtype),
        in_specs=[pl.BlockSpec(memory_space=pltpu.SMEM), vmem, vmem, vmem],
        out_specs=vmem,
        scratch_shapes=[
            pltpu.VMEM((levels, GROUP, REACH + 2, bs, bs), BF16),
            pltpu.VMEM((levels - 1, REACH + GROUP, bs, width), BF16),
            pltpu.VMEM((levels, GROUP, bs, width), BF16),
            pltpu.VMEM((levels, GROUP, width, bs), BF16),
            pltpu.VMEM((levels, GROUP, width, bs), BF16),
            pltpu.VMEM((levels - 1, GROUP, width, bs), BF16),
            pltpu.VMEM((levels - 1, width, bs), BF16),
            pltpu.VMEM((levels - 1, REACH, width, bs), BF16),
            pltpu.VMEM((levels, GROUP, bs, width), BF16),
            dma((levels, 2)), dma((levels, 2)),
            dma((levels, 2)), dma((levels, 2)),
            dma((levels, 4, ncores - 1)), dma((levels, 4, ncores - 1)),
            dma((levels, 3)), dma((levels, 3)), dma((levels,)),
            dma((levels - 1, REACH)), dma((levels - 1, REACH)),
            dma((levels - 1, REACH)), dma((levels - 1, REACH)),
            dma((levels, 4)), dma((levels, 3)),
        ],
        compiler_params=pltpu.CompilerParams(
            collective_id=0, has_side_effects=True, vmem_limit_bytes=48 << 20
        ),
    )(neighbours[:, 0], rhs, blocks, diag_inv)


def solution(mesh):
    placed = (
        P(None, "sweep", None, "cols"),
        P(None, "sweep", None, "cols", None),
        P(None, "sweep", "cols", None),
        P(None, "sweep", None),
    )
    return jax.shard_map(
        on_device,
        mesh=mesh,
        in_specs=placed,
        out_specs=P(None, "sweep", None, "cols"),
        check_vma=False,
    )
```
